32 devices in a mesh: parts: 2 (over y), blk: 8 (over z, x), sub: 2 (over core).
Axes of the slice: x: 2, y: 2, z: 4, core: 2. Of those that a mesh axis runs over, the one named last changes fastest.
Arguments:
- embeddings: bfloat16 [24576, 1024], P(('parts', 'blk', 'sub')), parts along dimension 0, may hold values from -6 to 6
- labels: int32 [24576], P(('parts', 'blk', 'sub')), parts along dimension 0, may hold values from 0 to 127, as said below
Outputs:
- dedup_weight: float32 [24576], P(('parts', 'blk', 'sub')), parts along dimension 0
- cluster_mass: float32 [256], P('parts'), parts along dimension 0
The draws below stay inside these ranges and needn't reach their ends.
There are 2 independent parts, one for each index of `parts`. The reference program is written for one: setup_inputs(seed, part) draws one part's arguments, and reference() takes and returns one part's arrays. A program takes and returns all parts, laid end to end along the dimension named above; each array names one. Nothing has to cross between parts.
Inputs may be any that keep to these rules, and one draw needn't show every extreme that they name: `labels`: every label of 0 to 127 occurs.
All inputs are finite; a program needn't handle non-finite values.
Results may differ from the reference program's by a relative error of at most 0.0003.
Values may be sent and summed in bfloat16 or wider, within the bound.
No kernel may reach another device: no remote copies, remote signals or barrier semaphores. Data moves between devices by JAX's collectives and lax.ppermute only.
A program may use at most 64 MiB of HBM per device.

```python
import math
import jax
import jax.numpy as jnp
from jax import lax

D = 1024
CLUSTERS = 128
ROUNDS = 3
BLOCK = 1536
ROWS = 12288


def common_groups(key):
    group = BLOCK * (ROUNDS + 1)
    fam_per = max(1, group // 8)
    group_count = (ROWS + group - 1) // group
    family_count = group_count * fam_per
    positions = jnp.arange(ROWS, dtype=jnp.int32)
    family_rows = positions // group * fam_per + jax.random.randint(jax.random.fold_in(key, 21), (ROWS,), 0, fam_per)
    home_label = jax.random.randint(jax.random.fold_in(key, 22), (family_count,), 0, CLUSTERS)
    stray_label = jax.random.randint(jax.random.fold_in(key, 23), (ROWS,), 0, CLUSTERS)
    keeper = jax.random.randint(jax.random.fold_in(key, 24), (ROWS,), 0, 5) < 3
    label_rows = jnp.where(keeper, home_label[family_rows], stray_label)
    chosen = jax.random.permutation(jax.random.fold_in(key, 25), ROWS)[:CLUSTERS]
    label_rows = label_rows.at[chosen].set(jnp.arange(CLUSTERS, dtype=jnp.int32))
    return (label_rows.astype(jnp.int32), family_rows.astype(jnp.int32), family_count)


def draw_labels(key, part):
    label_rows, family_rows, family_count = common_groups(key)
    return label_rows


def draw_embeddings(key, part):
    label_rows, family_rows, family_count = common_groups(key)
    centers = jax.random.normal(jax.random.fold_in(key, 13), (CLUSTERS, D), jnp.float32)
    family_centers = jax.random.normal(jax.random.fold_in(key, 16), (family_count, D), jnp.float32)
    jitter = jax.random.normal(jax.random.fold_in(key, 14), (ROWS, D), jnp.float32)
    spread = jnp.exp(jax.random.uniform(jax.random.fold_in(key, 17), (ROWS,), jnp.float32, math.log(0.1), math.log(0.6)))
    values = 0.387 * centers[label_rows] + 0.922 * family_centers[family_rows] + spread[:, None] * jitter
    length = jnp.sqrt(jnp.sum(values * values, axis=1, keepdims=True))
    values = values * (math.sqrt(D) / length)
    return jnp.clip(values, -6.0, 6.0).astype(jnp.bfloat16)


def setup_inputs(seed: int = 0, part: int = 0) -> dict:
    key_of = jax.random.split(jax.random.key(seed), 3)
    own_keys = jax.random.split(jax.random.fold_in(key_of[2], part), 3)
    embeddings = draw_embeddings(jax.random.fold_in(jax.random.fold_in(key_of[2], part), 71), part)
    labels = draw_labels(jax.random.fold_in(jax.random.fold_in(key_of[2], part), 71), part)
    return {"embeddings": embeddings, "labels": labels}


TAU = 25.0


def kernel_rows(rows, row_lab, cols, col_lab):
    score = jnp.dot(rows, cols.T, preferred_element_type=jnp.float32) / D
    value = jnp.exp(TAU * (score - 1.0))
    value = jnp.where(row_lab[:, None] == col_lab[None, :], value, jnp.zeros_like(value))
    return jnp.sum(value, axis=1)


def reference(embeddings, labels):
    blocks = ROWS // BLOCK
    grouped = embeddings.reshape(blocks, BLOCK, D)
    grouped_lab = labels.reshape(blocks, BLOCK)

    def one_block(index):
        rows = grouped[index]
        row_lab = grouped_lab[index]
        total = kernel_rows(rows, row_lab, rows, row_lab)
        for mask in range(1, ROUNDS + 1):
            other = jnp.bitwise_xor(index, mask)
            total = total + kernel_rows(rows, row_lab, grouped[other], grouped_lab[other])
        return total

    density = lax.map(one_block, jnp.arange(blocks, dtype=jnp.int32))
    weight = 1.0 / density.reshape(ROWS)
    ident = jnp.arange(CLUSTERS, dtype=jnp.int32)
    mass = jnp.sum(jnp.where(labels[:, None] == ident[None, :], weight[:, None], jnp.zeros_like(weight)[:, None]), axis=0)
    return weight, mass
```

```python
import functools
import math

import jax
import jax.numpy as jnp
from jax import lax
from jax.experimental import pallas as pl
from jax.experimental.pallas import tpu as pltpu
from jax.sharding import PartitionSpec as P

CLUSTERS = 128
ROUNDS = 3
TAU = 25.0
LOG2E = math.log2(math.e)
AXES = ("blk", "sub")
LANES = 128


def exchange(value, xor):
    count = lax.axis_size("blk") * lax.axis_size("sub")
    return lax.ppermute(value, AXES, [(i, i ^ xor) for i in range(count)])


def exchange_flipped(value, chip_bit, flip):
    pairs = []
    for blk in range(lax.axis_size("blk")):
        for sub in range(2):
            source = (blk ^ (1 << chip_bit)) * 2 + (sub ^ flip(blk))
            pairs.append((source, blk * 2 + sub))
    return lax.ppermute(value, AXES, pairs)


def flip_x(blk):
    return (blk ^ (blk >> 1)) & 1


def flip_z(blk):
    return (blk >> 1) & 1


def values(rows, row_lab, cols, col_lab, width):
    scale = TAU * LOG2E / width
    score = lax.dot_general(rows, cols, (((1,), (1,)), ((), ())), preferred_element_type=jnp.float32)
    return jnp.where(row_lab == col_lab, jnp.exp2(score * scale - TAU * LOG2E), 0.0)


def add_tile(rows, row_lab, cols_ref, lab_ref, sum_ref, start, size, width, step):
    folded = jnp.zeros((rows.shape[0], LANES), jnp.float32)
    for at in range(0, size, step):
        there = slice(start + at, start + at + step)
        value = values(rows, row_lab, cols_ref[at : at + step, :], lab_ref[:, there], width)
        sum_ref[:, there] += jnp.sum(value, axis=0, keepdims=True)
        for lane in range(0, step, LANES):
            folded = folded + value[:, lane : lane + LANES]
    return folded


def to_lanes(folded):
    return jnp.sum(folded.T, axis=0, keepdims=True)


def near_kernel(own_ref, other_ref, own_col, other_col, own_row, out_ref, *, width, step):
    out_ref[...] = jnp.zeros_like(out_ref)
    count = own_ref.shape[0]
    for rows_ref, col in ((own_ref, own_col), (other_ref, other_col)):
        for at in range(0, count, step):
            value = values(rows_ref[...], col[...], own_ref[at : at + step, :], own_row[:, at : at + step], width)
            out_ref[:, at : at + step] += jnp.sum(value, axis=0, keepdims=True)


def near(own, other, own_col, other_col, own_row):
    count, width = own.shape
    return pl.pallas_call(
        functools.partial(near_kernel, width=width, step=256),
        out_shape=jax.ShapeDtypeStruct((1, count), jnp.float32),
        cost_estimate=pl.CostEstimate(
            flops=4 * count * count * width, bytes_accessed=4 * count * width, transcendentals=2 * count * count
        ),
    )(own, other, own_col, other_col, own_row)


def far_kernel(*refs, count, width, chunks):
    k = len(chunks) - 1
    xs, zs = refs[: k + 1], refs[k + 1 : 2 * k + 2]
    own, own_row, x_col, z_col, x_row, z_row, own_in, x_in, z_in, own_sum, x_sum, z_sum = refs[2 * k + 2 :]
    own_sum[...] = own_in[...]
    x_sum[...] = x_in[...]
    z_sum[...] = z_in[...]
    size = chunks[k]
    first = sum(chunks[:k])
    x_new, z_new = xs[k][...], zs[k][...]
    lab_x, lab_z = x_col[first : first + size], z_col[first : first + size]
    fold_x = add_tile(x_new, lab_x, own, own_row, own_sum, 0, count, width, min(count, 256))
    fold_z = add_tile(z_new, lab_z, own, own_row, own_sum, 0, count, width, min(count, 256))
    at = 0
    for j in range(k + 1):
        n = chunks[j]
        fold_x = fold_x + add_tile(x_new, lab_x, zs[j], z_row, z_sum, at, n, width, min(n, 256))
        if j < k:
            fold_z = fold_z + add_tile(z_new, lab_z, xs[j], x_row, x_sum, at, n, width, min(n, 256))
        at += n
    x_sum[:, first : first + size] += to_lanes(fold_x)
    z_sum[:, first : first + size] += to_lanes(fold_z)


def far(xs, zs, own, own_row, x_col, z_col, x_row, z_row, sums, chunks):
    count, width = own.shape
    k = len(xs) - 1
    pairs = 2 * chunks[k] * count + chunks[k] * (2 * sum(chunks[:k]) + chunks[k])
    return pl.pallas_call(
        functools.partial(far_kernel, count=count, width=width, chunks=tuple(chunks[: k + 1])),
        out_shape=[jax.ShapeDtypeStruct((1, count), jnp.float32)] * 3,
        cost_estimate=pl.CostEstimate(
            flops=2 * pairs * width, bytes_accessed=2 * width * (count + 2 * sum(chunks[: k + 1])), transcendentals=pairs
        ),
    )(*xs, *zs, own, own_row, x_col, z_col, x_row, z_row, *sums)


def cut(count):
    if count % 256 == 0 and count > 256:
        return [256] * (count // 256 - 1) + [128, 128]
    if count % 128 == 0:
        return [128] * (count // 128)
    return [count]


def per_device(embeddings, labels):
    count, width = embeddings.shape
    blk, sub = lax.axis_index("blk"), lax.axis_index("sub")
    chunks = cut(count)
    xs, zs = [], []
    at = 0
    chip_lab = None
    for n in chunks:
        piece = lax.slice_in_dim(embeddings, at, at + n, axis=0)
        xs.append(exchange_flipped(piece, 0, flip_x))
        zs.append(exchange_flipped(piece, 1, flip_z))
        at += n
    partner = exchange(embeddings, 1)
    lab = labels[None, :]
    lab_s = jnp.concatenate([lab, exchange(lab, 1)], axis=0)
    lab_x = exchange(lab_s, 2)
    lab_z = exchange(lab_s, 4)
    lab_d = exchange(lab_x, 4)
    lab_all = jnp.concatenate([lab_s, lab_x, lab_z, lab_d], axis=0)
    turn_x, turn_z = flip_x(blk) == 1, flip_z(blk) == 1
    x_lab = jnp.where(turn_x, lab_x[1:2], lab_x[0:1])
    z_lab = jnp.where(turn_z, lab_z[1:2], lab_z[0:1])

    col = lambda a: a.reshape(count, 1)
    own_sum = near(embeddings, partner, col(lab), col(lab_s[1:2]), lab)
    zero = jnp.zeros((1, count), jnp.float32)
    sums = (own_sum, zero, zero)
    for k in range(len(chunks)):
        sums = far(xs[: k + 1], zs[: k + 1], embeddings, lab, col(x_lab), col(z_lab), x_lab, z_lab, sums, chunks)

    own_sum, x_sum, z_sum = sums
    part = jnp.concatenate(
        [
            own_sum,
            zero,
            jnp.where(turn_x, zero, x_sum),
            jnp.where(turn_x, x_sum, zero),
            jnp.where(turn_z, zero, z_sum),
            jnp.where(turn_z, z_sum, zero),
            zero,
            zero,
        ],
        axis=0,
    )

    def turned(a, bit):
        return jnp.concatenate([a[r ^ bit : (r ^ bit) + 1] for r in range(8)], axis=0)

    for bit in (1, 2, 4):
        part = part + turned(exchange(part, bit), bit)
    weight = 1.0 / part
    ident = jnp.arange(CLUSTERS, dtype=jnp.int32)
    mass = jnp.sum(jnp.where(lab_all[:, None, :] == ident[None, :, None], weight[:, None, :], 0.0), axis=(0, 2))
    bit = 8
    while bit < lax.axis_size("blk") * 2:
        mass = mass + exchange(mass, bit)
        bit *= 2
    return weight[0], mass


def solution(mesh):
    in_specs = (P(("parts", "blk", "sub"), None), P(("parts", "blk", "sub")))
    out_specs = (P(("parts", "blk", "sub")), P("parts"))
    return jax.shard_map(per_device, mesh=mesh, in_specs=in_specs, out_specs=out_specs, check_vma=False)
```

```python
import functools
import math

import jax
import jax.numpy as jnp
from jax import lax
from jax.experimental import pallas as pl
from jax.experimental.pallas import tpu as pltpu
from jax.sharding import PartitionSpec as P

CLUSTERS = 128
TAU = 25.0
LOG2E = math.log2(math.e)
AXES = ("blk", "sub")
LANES = 128
VMEM = pl.BlockSpec(memory_space=pltpu.VMEM)
SMEM = pl.BlockSpec(memory_space=pltpu.SMEM)
PARAMS = pltpu.CompilerParams(vmem_limit_bytes=16 << 20)


def exchange(value, xor):
    count = lax.axis_size("blk") * lax.axis_size("sub")
    return lax.ppermute(value, AXES, [(i, i ^ xor) for i in range(count)])


def exchange_flipped(value, chip_bit, flip):
    pairs = []
    for blk in range(lax.axis_size("blk")):
        for sub in range(2):
            source = (blk ^ (1 << chip_bit)) * 2 + (sub ^ flip(blk))
            pairs.append((source, blk * 2 + sub))
    return lax.ppermute(value, AXES, pairs)


def flip_x(blk):
    return (blk ^ (blk >> 1)) & 1


def flip_z(blk):
    return (blk >> 1) & 1


def down_rows(lab, first, size):
    pieces = []
    for at in range(first, first + size, LANES):
        n = min(LANES, first + size - at)
        pieces.append(jnp.broadcast_to(lab[:, at : at + n], (LANES, n)).T)
    return pieces[0] if len(pieces) == 1 else jnp.concatenate(pieces, axis=0)


def tile(rows, down, cols_ref, lab_ref, sum_ref, start, size, width, step, fold=True):
    m = rows.shape[0]
    scale = TAU * LOG2E / width
    folded = jnp.zeros((m, LANES), jnp.float32)
    for at in range(0, size, step):
        n = min(step, size - at)
        score = lax.dot_general(
            rows, cols_ref[at : at + n, :], (((1,), (1,)), ((), ())), preferred_element_type=jnp.float32
        )
        power = jnp.exp2(score * scale - TAU * LOG2E)
        for lane in range(0, n, LANES):
            there = slice(start + at + lane, start + at + lane + LANES)
            value = jnp.where(down == lab_ref[:, there], power[:, lane : lane + LANES], 0.0)
            sum_ref[:, there] += jnp.sum(value, axis=0, keepdims=True)
            if fold:
                folded = folded + value
    return folded


def to_lanes(folded):
    return jnp.sum(folded.T, axis=0, keepdims=True)


def near_kernel(own_ref, other_ref, own_row, other_row, out_ref, *, width):
    out_ref[...] = jnp.zeros_like(out_ref)
    count = own_ref.shape[0]
    for rows_ref, lab in ((own_ref, own_row), (other_ref, other_row)):
        for at in range(0, count, 256):
            m = min(256, count - at)
            tile(rows_ref[at : at + m, :], down_rows(lab, at, m), own_ref, own_row, out_ref, 0, count, width, 256, False)


def near(own, other, own_row, other_row):
    count, width = own.shape
    return pl.pallas_call(
        functools.partial(near_kernel, width=width),
        out_shape=jax.ShapeDtypeStruct((1, count), jnp.float32),
        in_specs=[VMEM] * 4,
        out_specs=VMEM,
        compiler_params=PARAMS,
        cost_estimate=pl.CostEstimate(
            flops=4 * count * count * width, bytes_accessed=4 * count * width, transcendentals=2 * count * count
        ),
    )(own, other, own_row, other_row)


def far_kernel(*refs, count, width, chunks, last):
    k = len(chunks) - 1
    xs, zs = refs[: k + 1], refs[k + 1 : 2 * k + 2]
    own, own_row, x_row, z_row, own_in, x_in, z_in, turns = refs[2 * k + 2 : 2 * k + 10]
    outs = refs[2 * k + 10 :]
    own_sum, x_sum, z_sum = outs[-3:]
    own_sum[...] = own_in[...]
    x_sum[...] = x_in[...]
    z_sum[...] = z_in[...]
    size = chunks[k]
    first = sum(chunks[:k])
    x_new, z_new = xs[k][...], zs[k][...]
    down_x, down_z = down_rows(x_row, first, size), down_rows(z_row, first, size)
    fold_x = tile(x_new, down_x, own, own_row, own_sum, 0, count, width, 256)
    fold_z = tile(z_new, down_z, own, own_row, own_sum, 0, count, width, 256)
    at = 0
    for j in range(k + 1):
        n = chunks[j]
        fold_x = fold_x + tile(x_new, down_x, zs[j], z_row, z_sum, at, n, width, 256)
        if j < k:
            fold_z = fold_z + tile(z_new, down_z, xs[j], x_row, x_sum, at, n, width, 256)
        at += n
    x_sum[:, first : first + size] += to_lanes(fold_x)
    z_sum[:, first : first + size] += to_lanes(fold_z)
    if last:
        part = outs[0]
        zero = jnp.zeros((1, count), jnp.float32)
        turn_x, turn_z = turns[0] == 1, turns[1] == 1
        part[0:1, :] = own_sum[...]
        part[1:2, :] = zero
        part[2:3, :] = jnp.where(turn_x, zero, x_sum[...])
        part[3:4, :] = jnp.where(turn_x, x_sum[...], zero)
        part[4:5, :] = jnp.where(turn_z, zero, z_sum[...])
        part[5:6, :] = jnp.where(turn_z, z_sum[...], zero)
        part[6:7, :] = zero
        part[7:8, :] = zero


def far(xs, zs, own, own_row, x_row, z_row, sums, turns, chunks):
    count, width = own.shape
    k = len(xs) - 1
    last = k == len(chunks) - 1
    pairs = 2 * chunks[k] * count + chunks[k] * (2 * sum(chunks[:k]) + chunks[k])
    row = jax.ShapeDtypeStruct((1, count), jnp.float32)
    return pl.pallas_call(
        functools.partial(far_kernel, count=count, width=width, chunks=tuple(chunks[: k + 1]), last=last),
        out_shape=jax.ShapeDtypeStruct((8, count), jnp.float32) if last else [row] * 3,
        in_specs=[VMEM] * (2 * k + 9) + [SMEM],
        out_specs=VMEM if last else [VMEM] * 3,
        scratch_shapes=[pltpu.VMEM((1, count), jnp.float32)] * 3 if last else [],
        compiler_params=PARAMS,
        cost_estimate=pl.CostEstimate(
            flops=2 * pairs * width, bytes_accessed=2 * width * (count + 2 * sum(chunks[: k + 1])), transcendentals=pairs
        ),
    )(*xs, *zs, own, own_row, x_row, z_row, *sums, turns)


def cut(count):
    if count % 256 == 0 and count > 256:
        return [256] * (count // 256 - 1) + [128, 128]
    if count % 128 == 0:
        return [128] * (count // 128)
    return [count]


def per_device(embeddings, labels):
    count, _ = embeddings.shape
    blk = lax.axis_index("blk")
    chunks = cut(count)
    turns = jnp.stack([flip_x(blk), flip_z(blk)]).astype(jnp.int32)
    lab = labels[None, :]
    xs, zs = [], []

    def send(source, at, n):
        piece = lax.slice_in_dim(source, at, at + n, axis=0)
        xs.append(exchange_flipped(piece, 0, flip_x))
        zs.append(exchange_flipped(piece, 1, flip_z))

    send(embeddings, 0, chunks[0])
    other = exchange(lab, 1)
    lab_s = jnp.concatenate([lab, other], axis=0)
    lab_x = exchange(lab_s, 2)
    lab_z = exchange(lab_s, 4)
    source, lab_s, lab = lax.optimization_barrier((embeddings, lab_s, lab))
    at = chunks[0]
    for k, n in enumerate(chunks[1:], 1):
        send(source, at, n)
        at += n
    lab_d = exchange(lab_x, 4)
    partner = exchange(source, 1)
    lab_all = jnp.concatenate([lab_s, lab_x, lab_z, lab_d], axis=0)
    x_lab = jnp.where(turns[0] == 1, lab_x[1:2], lab_x[0:1])
    z_lab = jnp.where(turns[1] == 1, lab_z[1:2], lab_z[0:1])

    own_sum = near(embeddings, partner, lab, other)
    zero = jnp.zeros((1, count), jnp.float32)
    sums = (own_sum, zero, zero)
    for k in range(len(chunks)):
        sums = far(xs[: k + 1], zs[: k + 1], embeddings, lab, x_lab, z_lab, sums, turns, chunks)
    part = sums

    def turned(a, bit):
        return jnp.concatenate([a[r ^ bit : (r ^ bit) + 1] for r in range(8)], axis=0)

    for bit in (1, 2, 4):
        part = part + turned(exchange(part, bit), bit)
    weight = 1.0 / part
    ident = jnp.arange(CLUSTERS, dtype=jnp.int32)
    mass = jnp.sum(jnp.where(lab_all[:, None, :] == ident[None, :, None], weight[:, None, :], 0.0), axis=(0, 2))
    bit = 8
    while bit < lax.axis_size("blk") * 2:
        mass = mass + exchange(mass, bit)
        bit *= 2
    return weight[0], mass


def solution(mesh):
    in_specs = (P(("parts", "blk", "sub"), None), P(("parts", "blk", "sub")))
    out_specs = (P(("parts", "blk", "sub")), P("parts"))
    return jax.shard_map(per_device, mesh=mesh, in_specs=in_specs, out_specs=out_specs, check_vma=False)
```

```python
import functools
import math

import jax
import jax.numpy as jnp
from jax import lax
from jax.experimental import pallas as pl
from jax.experimental.pallas import tpu as pltpu
from jax.sharding import PartitionSpec as P

CLUSTERS = 128
TAU = 25.0
LOG2E = math.log2(math.e)
AXES = ("blk", "sub")
LANES = 128
VMEM = pl.BlockSpec(memory_space=pltpu.VMEM)
SMEM = pl.BlockSpec(memory_space=pltpu.SMEM)
PARAMS = pltpu.CompilerParams(vmem_limit_bytes=16 << 20)


def exchange(value, xor):
    count = lax.axis_size("blk") * lax.axis_size("sub")
    return lax.ppermute(value, AXES, [(i, i ^ xor) for i in range(count)])


def exchange_flipped(value, chip_bit, flip):
    pairs = []
    for blk in range(lax.axis_size("blk")):
        for sub in range(2):
            source = (blk ^ (1 << chip_bit)) * 2 + (sub ^ flip(blk))
            pairs.append((source, blk * 2 + sub))
    return lax.ppermute(value, AXES, pairs)


def flip_x(blk):
    return (blk ^ (blk >> 1)) & 1


def flip_z(blk):
    return (blk >> 1) & 1


def down_rows(lab, first, size):
    pieces = []
    for at in range(first, first + size, LANES):
        n = min(LANES, first + size - at)
        pieces.append(jnp.broadcast_to(lab[:, at : at + n], (LANES, n)).T)
    return pieces[0] if len(pieces) == 1 else jnp.concatenate(pieces, axis=0)


def tile(rows, down, cols_ref, lab_ref, sum_ref, line, start, size, width, fold=True):
    scale = TAU * LOG2E / width
    folded = jnp.zeros((rows.shape[0], LANES), jnp.float32)
    for at in range(0, size, 256):
        n = min(256, size - at)
        score = lax.dot_general(
            rows, cols_ref[at : at + n, :], (((1,), (1,)), ((), ())), preferred_element_type=jnp.float32
        )
        power = jnp.exp2(score * scale - TAU * LOG2E)
        for lane in range(0, n, LANES):
            there = slice(start + at + lane, start + at + lane + LANES)
            value = jnp.where(down == lab_ref[:, there], power[:, lane : lane + LANES], 0.0)
            sum_ref[line : line + 1, there] = sum_ref[line : line + 1, there] + jnp.sum(value, axis=0, keepdims=True)
            if fold:
                folded = folded + value
    return folded


def to_lanes(folded):
    return jnp.sum(folded.T, axis=0, keepdims=True)


def split_kernel(source, *rest, spans):
    outs, sem = rest[:-1], rest[-1]
    copies = [
        pltpu.make_async_copy(source.at[pl.ds(at, n)], out, sem.at[i]) for i, ((at, n), out) in enumerate(zip(spans, outs))
    ]
    for copy in copies:
        copy.start()
    for copy in copies:
        copy.wait()


def split(source, spans):
    width = source.shape[1]
    return pl.pallas_call(
        functools.partial(split_kernel, spans=tuple(spans)),
        out_shape=[jax.ShapeDtypeStruct((n, width), source.dtype) for _, n in spans],
        in_specs=[pl.BlockSpec(memory_space=pltpu.HBM)],
        out_specs=[VMEM] * len(spans),
        scratch_shapes=[pltpu.SemaphoreType.DMA((len(spans),))],
        compiler_params=PARAMS,
        cost_estimate=pl.CostEstimate(flops=0, bytes_accessed=4 * width * sum(n for _, n in spans), transcendentals=0),
    )(source)


def near_kernel(*refs, width, chunks):
    pieces = refs[: len(chunks)]
    other_ref, own_row, other_row, out_ref = refs[len(chunks) :]
    out_ref[...] = jnp.zeros_like(out_ref)
    count = sum(chunks)
    rows = [(piece, own_row, 0, at, n) for piece, at, n in zip(pieces, starts(chunks), chunks)]
    rows += [(other_ref, other_row, at, at, min(256, count - at)) for at in range(0, count, 256)]
    for ref, lab, inner, at, m in rows:
        down = down_rows(lab, at, m)
        for piece, start, n in zip(pieces, starts(chunks), chunks):
            tile(ref[inner : inner + m, :], down, piece, own_row, out_ref, 0, start, n, width, False)


def starts(chunks):
    return [sum(chunks[:k]) for k in range(len(chunks))]


def near(own, other, own_row, other_row, chunks):
    count, width = other.shape
    return pl.pallas_call(
        functools.partial(near_kernel, width=width, chunks=tuple(chunks)),
        out_shape=jax.ShapeDtypeStruct((3, count), jnp.float32),
        in_specs=[VMEM] * (len(own) + 3),
        out_specs=VMEM,
        compiler_params=PARAMS,
        cost_estimate=pl.CostEstimate(
            flops=4 * count * count * width, bytes_accessed=4 * count * width, transcendentals=2 * count * count
        ),
    )(*own, other, own_row, other_row)


def far_kernel(*refs, width, chunks, xn, zn, new):
    parts = len(chunks)
    own, refs = refs[:parts], refs[parts:]
    xs, zs = refs[:xn], refs[xn : xn + zn]
    own_row, x_row, z_row, before, sums = refs[xn + zn :]
    rows = {"x": x_row, "z": z_row}
    at = starts(chunks)
    sums[...] = before[...]
    fresh = []
    for way in new:
        k = (xn if way == "x" else zn) - 1
        piece = (xs if way == "x" else zs)[k]
        fresh.append((way, k, piece[...], down_rows(rows[way], at[k], chunks[k])))
    all_rows = fresh[0][2] if len(fresh) == 1 else jnp.concatenate([f[2] for f in fresh], axis=0)
    all_down = fresh[0][3] if len(fresh) == 1 else jnp.concatenate([f[3] for f in fresh], axis=0)
    fold = jnp.zeros((all_rows.shape[0], LANES), jnp.float32)
    for j in range(parts):
        fold = fold + tile(all_rows, all_down, own[j], own_row, sums, 0, at[j], chunks[j], width)
    first = 0
    for way, k, piece, down in fresh:
        mine, others, other_row, line = (1, zs, z_row, 2) if way == "x" else (2, xs, x_row, 1)
        if way == "z" and "x" in new:
            others = others[:-1]
        part = fold[first : first + chunks[k]]
        for j in range(len(others)):
            part = part + tile(piece, down, others[j], other_row, sums, line, at[j], chunks[j], width)
        there = slice(at[k], at[k] + chunks[k])
        sums[mine : mine + 1, there] = sums[mine : mine + 1, there] + to_lanes(part)
        first += chunks[k]


def far(own, xs, zs, own_row, x_row, z_row, sums, chunks, new):
    width, count = own[0].shape[1], sum(chunks)
    n = chunks[len(xs) - 1 if "x" in new else len(zs) - 1]
    pairs = n * len(new) * (count + sum(chunks[: len(xs)]))
    return pl.pallas_call(
        functools.partial(far_kernel, width=width, chunks=tuple(chunks), xn=len(xs), zn=len(zs), new=new),
        out_shape=jax.ShapeDtypeStruct(sums.shape, jnp.float32),
        in_specs=[VMEM] * (len(own) + len(xs) + len(zs) + 4),
        out_specs=VMEM,
        compiler_params=PARAMS,
        cost_estimate=pl.CostEstimate(
            flops=2 * pairs * width, bytes_accessed=2 * width * (count + sum(chunks)), transcendentals=pairs
        ),
    )(*own, *xs, *zs, own_row, x_row, z_row, sums)


CHUNKS = 4


def cut(count):
    tiles = count // LANES
    base, more = divmod(tiles - 1, CHUNKS - 1)
    return [(base + (k < more)) * LANES for k in range(CHUNKS - 1)] + [LANES]


def per_device(embeddings, labels):
    count, _ = embeddings.shape
    blk = lax.axis_index("blk")
    chunks = cut(count)
    turns = jnp.stack([flip_x(blk), flip_z(blk)]).astype(jnp.int32)
    xs, zs = [], []

    def send(piece):
        xs.append(exchange_flipped(piece, 0, flip_x))
        zs.append(exchange_flipped(piece, 1, flip_z))

    spans = list(zip(starts(chunks), chunks))
    own = split(embeddings, spans[:1])
    send(own[0])
    lab = labels[None, :]
    other = exchange(lab, 1)
    lab_s = jnp.concatenate([lab, other], axis=0)
    lab_x = exchange(lab_s, 2)
    lab_z = exchange(lab_s, 4)
    source, lab = lax.optimization_barrier((embeddings, lab))
    if len(chunks) > 1:
        own = own + split(source, spans[1:])
    for k in range(1, len(chunks)):
        send(own[k])
    lab_d = exchange(lab_x, 4)
    partner = exchange(source, 1)
    lab_all = jnp.concatenate([lab_s, lab_x, lab_z, lab_d], axis=0)
    x_lab = jnp.where(turns[0] == 1, lab_x[1:2], lab_x[0:1])
    z_lab = jnp.where(turns[1] == 1, lab_z[1:2], lab_z[0:1])
    sums = near(own, partner, lab, other, chunks)
    last = len(chunks)
    for k in range(1, last):
        sums = far(own, xs[:k], zs[:k], lab, x_lab, z_lab, sums, chunks, "xz")
    sums = far(own, xs, zs[:-1], lab, x_lab, z_lab, sums, chunks, "x")
    sums = far(own, xs, zs, lab, x_lab, z_lab, sums, chunks, "z")
    ax, bz = turns[0] == 1, turns[1] == 1
    part = spread3(sums, ax, bz) + turned(spread3(exchange(sums, 3), ~ax, bz), 3)
    six = jnp.concatenate([part[0:4], jnp.where(bz, part[5:6], part[4:5]), jnp.where(bz, part[6:7], part[7:8])], axis=0)
    part = part + turned(spread6(exchange(six, 5), ~bz), 5)
    part = part + turned(exchange(part, 1), 1)
    weight = 1.0 / part
    ident = jnp.arange(CLUSTERS, dtype=jnp.int32)
    mass = jnp.sum(jnp.where(lab_all[:, None, :] == ident[None, :, None], weight[:, None, :], 0.0), axis=(0, 2))
    bit = 8
    while bit < lax.axis_size("blk") * 2:
        mass = mass + exchange(mass, bit + 1)
        bit *= 2
    return weight[0], mass


def turned(rows, xor):
    return jnp.concatenate([rows[r ^ xor : (r ^ xor) + 1] for r in range(8)], axis=0)


def spread3(sums, ax, bz):
    own, x, z = sums[0:1], sums[1:2], sums[2:3]
    zero = jnp.zeros_like(own)
    return jnp.concatenate(
        [own, zero, jnp.where(ax, zero, x), jnp.where(ax, x, zero), jnp.where(bz, zero, z), jnp.where(bz, z, zero), zero, zero],
        axis=0,
    )


def spread6(six, bz):
    z, d = six[4:5], six[5:6]
    zero = jnp.zeros_like(z)
    return jnp.concatenate(
        [six[0:4], jnp.where(bz, zero, z), jnp.where(bz, z, zero), jnp.where(bz, d, zero), jnp.where(bz, zero, d)], axis=0
    )


def solution(mesh):
    in_specs = (P(("parts", "blk", "sub"), None), P(("parts", "blk", "sub")))
    out_specs = (P(("parts", "blk", "sub")), P("parts"))
    return jax.shard_map(per_device, mesh=mesh, in_specs=in_specs, out_specs=out_specs, check_vma=False)
```

```python
import functools
import math

import jax
import jax.numpy as jnp
from jax import lax
from jax.experimental import pallas as pl
from jax.experimental.pallas import tpu as pltpu
from jax.sharding import PartitionSpec as P

CLUSTERS = 128
TAU = 25.0
LOG2E = math.log2(math.e)
AXES = ("blk", "sub")
LANES = 128
VMEM = pl.BlockSpec(memory_space=pltpu.VMEM)
SMEM = pl.BlockSpec(memory_space=pltpu.SMEM)
PARAMS = pltpu.CompilerParams(vmem_limit_bytes=16 << 20)


def exchange(value, xor):
    count = lax.axis_size("blk") * lax.axis_size("sub")
    return lax.ppermute(value, AXES, [(i, i ^ xor) for i in range(count)])


def exchange_mixed(value):
    count = lax.axis_size("blk") * lax.axis_size("sub")
    return lax.ppermute(value, AXES, [(i, i ^ 2 if i & 1 else i ^ 4) for i in range(count)])


def down_rows(lab, first, size):
    pieces = []
    for at in range(first, first + size, LANES):
        n = min(LANES, first + size - at)
        pieces.append(jnp.broadcast_to(lab[:, at : at + n], (LANES, n)).T)
    return pieces[0] if len(pieces) == 1 else jnp.concatenate(pieces, axis=0)


def tile(rows, down, cols_ref, lab_ref, sum_ref, line, start, size, width, fold=True):
    scale = TAU * LOG2E / width
    folded = jnp.zeros((rows.shape[0], LANES), jnp.float32)
    for at in range(0, size, 256):
        n = min(256, size - at)
        score = lax.dot_general(
            rows, cols_ref[at : at + n, :], (((1,), (1,)), ((), ())), preferred_element_type=jnp.float32
        )
        power = jnp.exp2(score * scale - TAU * LOG2E)
        for lane in range(0, n, LANES):
            there = slice(start + at + lane, start + at + lane + LANES)
            value = jnp.where(down == lab_ref[:, there], power[:, lane : lane + LANES], 0.0)
            sum_ref[line : line + 1, there] = sum_ref[line : line + 1, there] + jnp.sum(value, axis=0, keepdims=True)
            if fold:
                folded = folded + value
    return folded


def to_lanes(folded):
    return jnp.sum(folded.T, axis=0, keepdims=True)


def split_kernel(source, *rest, spans):
    outs, sem = rest[:-1], rest[-1]
    copies = [
        pltpu.make_async_copy(source.at[pl.ds(at, n)], out, sem.at[i]) for i, ((at, n), out) in enumerate(zip(spans, outs))
    ]
    for copy in copies:
        copy.start()
    for copy in copies:
        copy.wait()


def split(source, spans):
    width = source.shape[1]
    return pl.pallas_call(
        functools.partial(split_kernel, spans=tuple(spans)),
        out_shape=[jax.ShapeDtypeStruct((n, width), source.dtype) for _, n in spans],
        in_specs=[pl.BlockSpec(memory_space=pltpu.HBM)],
        out_specs=[VMEM] * len(spans),
        scratch_shapes=[pltpu.SemaphoreType.DMA((len(spans),))],
        compiler_params=PARAMS,
        cost_estimate=pl.CostEstimate(flops=0, bytes_accessed=4 * width * sum(n for _, n in spans), transcendentals=0),
    )(source)


def near_kernel(*refs, width, chunks):
    parts = len(chunks)
    own, other = refs[:parts], refs[parts : 2 * parts]
    own_row, other_row, out_ref = refs[2 * parts :]
    out_ref[...] = jnp.zeros_like(out_ref)
    for pieces, lab in ((own, own_row), (other, other_row)):
        for rows, first, m in zip(pieces, starts(chunks), chunks):
            down = down_rows(lab, first, m)
            for piece, at, n in zip(own, starts(chunks), chunks):
                tile(rows[...], down, piece, own_row, out_ref, 0, at, n, width, False)


def starts(chunks):
    return [sum(chunks[:k]) for k in range(len(chunks))]


def near(own, other, own_row, other_row, chunks):
    width, count = own[0].shape[1], sum(chunks)
    return pl.pallas_call(
        functools.partial(near_kernel, width=width, chunks=tuple(chunks)),
        out_shape=jax.ShapeDtypeStruct((6, count), jnp.float32),
        in_specs=[VMEM] * (2 * len(own) + 2),
        out_specs=VMEM,
        compiler_params=PARAMS,
        cost_estimate=pl.CostEstimate(
            flops=4 * count * count * width, bytes_accessed=4 * count * width, transcendentals=2 * count * count
        ),
    )(*own, *other, own_row, other_row)


_, MET_FIRST, MET_SECOND, FIRST, SECOND, CROSS = range(6)


def far_kernel(*refs, width, chunks, news, ks, groups, line):
    parts = len(chunks)
    new, refs = refs[:news], refs[news:]
    cols = [refs[parts * g : parts * (g + 1)] for g in range(len(groups))]
    refs = refs[parts * len(groups) :]
    new_row, col_rows, (before, sums) = refs[0], refs[1 : 1 + len(groups)], refs[1 + len(groups) :]
    sums[...] = before[...]
    for piece, k in zip(new, ks):
        first, n = starts(chunks)[k], chunks[k]
        rows, down = piece[...], down_rows(new_row, first, n)
        fold = jnp.zeros((n, LANES), jnp.float32)
        for pieces, lab, met in zip(cols, col_rows, groups):
            for part, at, size in zip(pieces, starts(chunks), chunks):
                fold = fold + tile(rows, down, part, lab, sums, met, at, size, width)
        sums[line : line + 1, first : first + n] = sums[line : line + 1, first : first + n] + to_lanes(fold)


def far(new, ks, new_row, groups, sums, chunks, line):
    width, count = new[0].shape[1], sum(chunks)
    pairs = sum(chunks[k] for k in ks) * count * len(groups)
    cols = [piece for pieces, _, _ in groups for piece in pieces]
    return pl.pallas_call(
        functools.partial(
            far_kernel, width=width, chunks=tuple(chunks), news=len(new), ks=tuple(ks), groups=tuple(g[2] for g in groups), line=line
        ),
        out_shape=jax.ShapeDtypeStruct(sums.shape, jnp.float32),
        in_specs=[VMEM] * (len(new) + len(cols) + len(groups) + 2),
        out_specs=VMEM,
        compiler_params=PARAMS,
        cost_estimate=pl.CostEstimate(
            flops=2 * pairs * width, bytes_accessed=2 * width * count * (1 + len(groups)), transcendentals=pairs
        ),
    )(*new, *cols, new_row, *(g[1] for g in groups), sums)


def cut(count):
    tiles = count // LANES - 1
    return [tiles // 2 * LANES, (tiles - tiles // 2) * LANES, LANES]


def per_device(embeddings, labels):
    count, _ = embeddings.shape
    blk, sub = lax.axis_index("blk"), lax.axis_index("sub")
    chunks = cut(count)
    one = sub == 1
    low, high = blk & 1, (blk >> 1) & 1
    swapped, late = jnp.where(one, low, high) == 1, sub != high
    embeddings, labels, swapped, late, one, nil = lax.optimization_barrier((embeddings, labels, swapped, late, one, sub == 0))
    spans = list(zip(starts(chunks), chunks))
    first, second, cross = [], [], []
    own = [lax.slice_in_dim(embeddings, 0, chunks[0], axis=0)]
    first.append(exchange_mixed(own[0]))
    lab = labels[None, :]
    lab_other = exchange(lab, 1)
    lab_s = jnp.concatenate([lab, lab_other], axis=0)
    lab_x = exchange(lab_s, 2)
    lab_z = exchange(lab_s, 4)
    lab_d = exchange(lab_x, 4)
    source, _ = lax.optimization_barrier((embeddings, own[0]))
    own = own + list(split(source, spans[1:]))
    for k in range(1, len(chunks)):
        first.append(exchange_mixed(own[k]))
    partner = exchange(source, 1)
    other = split(partner, spans)
    for k in range(len(chunks)):
        second.append(exchange_mixed(other[k]))
    for k in range(len(chunks)):
        cross.append(exchange(first[k], 1))
    lab_all = jnp.concatenate([lab_s, lab_x, lab_z, lab_d], axis=0)
    first_lab, second_lab = jnp.where(one, lab_x[0:1], lab_z[0:1]), jnp.where(one, lab_x[1:2], lab_z[1:2])
    cross_lab = jnp.where(one, lab_z[1:2], lab_x[1:2])
    nobody = jnp.full_like(lab, -1)
    met_first = [jnp.where(swapped, b, a) for a, b in zip(own, other)]
    met_second = [jnp.where(swapped, a, b) for a, b in zip(own, other)]
    met_first_lab, met_second_lab = jnp.where(swapped, lab_other, lab), jnp.where(swapped, lab, lab_other)
    sums = near(own, other, lab, lab_other, chunks)
    for k in range(len(chunks)):
        sums = far(first[k : k + 1], [k], first_lab, [(met_first, met_first_lab, MET_FIRST)], sums, chunks, FIRST)
    early = [(cross, jnp.where(late, nobody, cross_lab), CROSS)]
    sums = far(first, range(len(chunks)), first_lab, early, sums, chunks, FIRST)
    meets = [(met_second, met_second_lab, MET_SECOND), (cross, jnp.where(late, cross_lab, nobody), CROSS)]
    for k in range(len(chunks)):
        sums = far(second[k : k + 1], [k], second_lab, meets, sums, chunks, SECOND)
    own_sum, met_a, met_b = sums[0:1], sums[1:2], sums[2:3]
    sums = jnp.concatenate(
        [own_sum + jnp.where(swapped, met_b, met_a), jnp.where(swapped, met_a, met_b), sums[3:6]], axis=0
    )
    part = spread(sums, one) + turned(spread(exchange(sums, 1), nil), 1)
    met = exchange(part[0:6], 3)
    part = part + turned(jnp.concatenate([met, jnp.zeros((2, count), jnp.float32)], axis=0), 3)
    part = part + turned(exchange(part, 5), 5)
    weight = 1.0 / part
    ident = jnp.arange(CLUSTERS, dtype=jnp.int32)
    mass = jnp.sum(jnp.where(lab_all[:, None, :] == ident[None, :, None], weight[:, None, :], 0.0), axis=(0, 2))
    bit = 8
    while bit < lax.axis_size("blk") * 2:
        mass = mass + exchange(mass, bit + 1)
        bit *= 2
    return weight[0], mass


def turned(rows, xor):
    return jnp.concatenate([rows[r ^ xor : (r ^ xor) + 1] for r in range(8)], axis=0)


def spread(sums, one):
    own, other, first, second, cross = (sums[r : r + 1] for r in range(5))
    zero = jnp.zeros_like(own)
    return jnp.concatenate(
        [
            own,
            other,
            jnp.where(one, first, zero),
            jnp.where(one, second, cross),
            jnp.where(one, zero, first),
            jnp.where(one, cross, second),
            zero,
            zero,
        ],
        axis=0,
    )


def solution(mesh):
    in_specs = (P(("parts", "blk", "sub"), None), P(("parts", "blk", "sub")))
    out_specs = (P(("parts", "blk", "sub")), P("parts"))
    return jax.shard_map(per_device, mesh=mesh, in_specs=in_specs, out_specs=out_specs, check_vma=False)
```

```python
import functools
import math

import jax
import jax.numpy as jnp
from jax import lax
from jax.experimental import pallas as pl
from jax.experimental.pallas import tpu as pltpu
from jax.sharding import PartitionSpec as P

CLUSTERS = 128
TAU = 25.0
LOG2E = math.log2(math.e)
AXES = ("blk", "sub")
LANES = 128
VMEM = pl.BlockSpec(memory_space=pltpu.VMEM)
SMEM = pl.BlockSpec(memory_space=pltpu.SMEM)
PARAMS = pltpu.CompilerParams(vmem_limit_bytes=16 << 20)


def exchange(value, xor):
    count = lax.axis_size("blk") * lax.axis_size("sub")
    return lax.ppermute(value, AXES, [(i, i ^ xor) for i in range(count)])


def exchange_mixed(value):
    count = lax.axis_size("blk") * lax.axis_size("sub")
    return lax.ppermute(value, AXES, [(i, i ^ 3 if i & 1 else i ^ 5) for i in range(count)])


def down_rows(lab, first, size):
    pieces = []
    for at in range(first, first + size, LANES):
        n = min(LANES, first + size - at)
        pieces.append(jnp.broadcast_to(lab[:, at : at + n], (LANES, n)).T)
    return pieces[0] if len(pieces) == 1 else jnp.concatenate(pieces, axis=0)


def tile(rows, down, cols_ref, lab_ref, sum_ref, line, start, size, width, fold=True):
    scale = TAU * LOG2E / width
    folded = jnp.zeros((rows.shape[0], LANES), jnp.float32)
    for at in range(0, size, 256):
        n = min(256, size - at)
        score = lax.dot_general(
            rows, cols_ref[at : at + n, :], (((1,), (1,)), ((), ())), preferred_element_type=jnp.float32
        )
        power = jnp.exp2(score * scale - TAU * LOG2E)
        for lane in range(0, n, LANES):
            there = slice(start + at + lane, start + at + lane + LANES)
            value = jnp.where(down == lab_ref[:, there], power[:, lane : lane + LANES], 0.0)
            sum_ref[line : line + 1, there] = sum_ref[line : line + 1, there] + jnp.sum(value, axis=0, keepdims=True)
            if fold:
                folded = folded + value
    return folded


def to_lanes(folded):
    return jnp.sum(folded.T, axis=0, keepdims=True)


def split_kernel(source, *rest, spans):
    outs, sem = rest[:-1], rest[-1]
    copies = [
        pltpu.make_async_copy(source.at[pl.ds(at, n)], out, sem.at[i]) for i, ((at, n), out) in enumerate(zip(spans, outs))
    ]
    for copy in copies:
        copy.start()
    for copy in copies:
        copy.wait()


def split(source, spans):
    width = source.shape[1]
    return pl.pallas_call(
        functools.partial(split_kernel, spans=tuple(spans)),
        out_shape=[jax.ShapeDtypeStruct((n, width), source.dtype) for _, n in spans],
        in_specs=[pl.BlockSpec(memory_space=pltpu.HBM)],
        out_specs=[VMEM] * len(spans),
        scratch_shapes=[pltpu.SemaphoreType.DMA((len(spans),))],
        compiler_params=PARAMS,
        cost_estimate=pl.CostEstimate(flops=0, bytes_accessed=4 * width * sum(n for _, n in spans), transcendentals=0),
    )(source)


def near_kernel(*refs, width, chunks):
    parts = len(chunks)
    own, other = refs[:parts], refs[parts : 2 * parts]
    own_row, other_row, out_ref = refs[2 * parts :]
    out_ref[...] = jnp.zeros_like(out_ref)
    for pieces, lab in ((own, own_row), (other, other_row)):
        for rows, first, m in zip(pieces, starts(chunks), chunks):
            down = down_rows(lab, first, m)
            for piece, at, n in zip(own, starts(chunks), chunks):
                tile(rows[...], down, piece, own_row, out_ref, 0, at, n, width, False)


def starts(chunks):
    return [sum(chunks[:k]) for k in range(len(chunks))]


def near(own, other, own_row, other_row, chunks):
    width, count = own[0].shape[1], sum(chunks)
    return pl.pallas_call(
        functools.partial(near_kernel, width=width, chunks=tuple(chunks)),
        out_shape=jax.ShapeDtypeStruct((6, count), jnp.float32),
        in_specs=[VMEM] * (2 * len(own) + 2),
        out_specs=VMEM,
        compiler_params=PARAMS,
        cost_estimate=pl.CostEstimate(
            flops=4 * count * count * width, bytes_accessed=4 * count * width, transcendentals=2 * count * count
        ),
    )(*own, *other, own_row, other_row)


_, MET_FIRST, MET_SECOND, FIRST, SECOND, CROSS = range(6)


def far_kernel(*refs, width, chunks, news, ks, groups, line):
    parts = len(chunks)
    new, refs = refs[:news], refs[news:]
    cols = [refs[parts * g : parts * (g + 1)] for g in range(len(groups))]
    refs = refs[parts * len(groups) :]
    new_row, col_rows, (before, sums) = refs[0], refs[1 : 1 + len(groups)], refs[1 + len(groups) :]
    sums[...] = before[...]
    for piece, k in zip(new, ks):
        first, n = starts(chunks)[k], chunks[k]
        rows, down = piece[...], down_rows(new_row, first, n)
        fold = jnp.zeros((n, LANES), jnp.float32)
        for pieces, lab, met in zip(cols, col_rows, groups):
            for part, at, size in zip(pieces, starts(chunks), chunks):
                fold = fold + tile(rows, down, part, lab, sums, met, at, size, width)
        sums[line : line + 1, first : first + n] = sums[line : line + 1, first : first + n] + to_lanes(fold)


def far(new, ks, new_row, groups, sums, chunks, line):
    width, count = new[0].shape[1], sum(chunks)
    pairs = sum(chunks[k] for k in ks) * count * len(groups)
    cols = [piece for pieces, _, _ in groups for piece in pieces]
    return pl.pallas_call(
        functools.partial(
            far_kernel, width=width, chunks=tuple(chunks), news=len(new), ks=tuple(ks), groups=tuple(g[2] for g in groups), line=line
        ),
        out_shape=jax.ShapeDtypeStruct(sums.shape, jnp.float32),
        in_specs=[VMEM] * (len(new) + len(cols) + len(groups) + 2),
        out_specs=VMEM,
        compiler_params=PARAMS,
        cost_estimate=pl.CostEstimate(
            flops=2 * pairs * width, bytes_accessed=2 * width * count * (1 + len(groups)), transcendentals=pairs
        ),
    )(*new, *cols, new_row, *(g[1] for g in groups), sums)


def cut(count):
    tiles = count // LANES - 1
    return [tiles // 2 * LANES, (tiles - tiles // 2) * LANES, LANES]


def per_device(embeddings, labels):
    count, _ = embeddings.shape
    blk, sub = lax.axis_index("blk"), lax.axis_index("sub")
    chunks = cut(count)
    one = sub == 1
    low, high = blk & 1, (blk >> 1) & 1
    swapped, late = jnp.where(one, high, low) == 0, sub == high
    embeddings, labels, swapped, late, one, nil = lax.optimization_barrier((embeddings, labels, swapped, late, one, sub == 0))
    spans = list(zip(starts(chunks), chunks))
    first, second, cross = [], [], []
    own = [lax.slice_in_dim(embeddings, 0, chunks[0], axis=0)]
    first.append(exchange_mixed(own[0]))
    lab = labels[None, :]
    lab_other = exchange(lab, 1)
    lab_s = jnp.concatenate([lab, lab_other], axis=0)
    lab_x = exchange(lab_s, 2)
    lab_z = exchange(lab_s, 4)
    lab_d = exchange(lab_x, 4)
    source, _ = lax.optimization_barrier((embeddings, own[0]))
    own = own + list(split(source, spans[1:]))
    for k in range(1, len(chunks)):
        first.append(exchange_mixed(own[k]))
    partner = exchange(source, 1)
    other = split(partner, spans)
    for k in range(len(chunks)):
        second.append(exchange_mixed(other[k]))
    for k in range(len(chunks)):
        cross.append(exchange(first[k], 1))
    lab_all = jnp.concatenate([lab_s, lab_x, lab_z, lab_d], axis=0)
    first_lab, second_lab = jnp.where(one, lab_z[1:2], lab_x[1:2]), jnp.where(one, lab_z[0:1], lab_x[0:1])
    cross_lab = jnp.where(one, lab_x[0:1], lab_z[0:1])
    nobody = jnp.full_like(lab, -1)
    met_first = [jnp.where(swapped, b, a) for a, b in zip(own, other)]
    met_second = [jnp.where(swapped, a, b) for a, b in zip(own, other)]
    met_first_lab, met_second_lab = jnp.where(swapped, lab_other, lab), jnp.where(swapped, lab, lab_other)
    sums = near(own, other, lab, lab_other, chunks)
    for k in range(len(chunks)):
        sums = far(first[k : k + 1], [k], first_lab, [(met_first, met_first_lab, MET_FIRST)], sums, chunks, FIRST)
    early = [(cross, jnp.where(late, nobody, cross_lab), CROSS)]
    sums = far(first, range(len(chunks)), first_lab, early, sums, chunks, FIRST)
    meets = [(met_second, met_second_lab, MET_SECOND), (cross, jnp.where(late, cross_lab, nobody), CROSS)]
    for k in range(len(chunks)):
        sums = far(second[k : k + 1], [k], second_lab, meets, sums, chunks, SECOND)
    own_sum, met_a, met_b = sums[0:1], sums[1:2], sums[2:3]
    sums = jnp.concatenate(
        [own_sum + jnp.where(swapped, met_b, met_a), jnp.where(swapped, met_a, met_b), sums[3:6]], axis=0
    )
    part = spread(sums, one) + turned(spread(exchange(sums, 1), nil), 1)
    met = exchange(part[0:6], 3)
    part = part + turned(jnp.concatenate([met, jnp.zeros((2, count), jnp.float32)], axis=0), 3)
    part = part + turned(exchange(part, 5), 5)
    weight = 1.0 / part
    ident = jnp.arange(CLUSTERS, dtype=jnp.int32)
    mass = jnp.sum(jnp.where(lab_all[:, None, :] == ident[None, :, None], weight[:, None, :], 0.0), axis=(0, 2))
    bit = 8
    while bit < lax.axis_size("blk") * 2:
        mass = mass + exchange(mass, bit + 1)
        bit *= 2
    return weight[0], mass


def turned(rows, xor):
    return jnp.concatenate([rows[r ^ xor : (r ^ xor) + 1] for r in range(8)], axis=0)


def spread(sums, one):
    own, other, first, second, cross = (sums[r : r + 1] for r in range(5))
    zero = jnp.zeros_like(own)
    return jnp.concatenate(
        [
            own,
            other,
            jnp.where(one, cross, second),
            jnp.where(one, zero, first),
            jnp.where(one, second, cross),
            jnp.where(one, first, zero),
            zero,
            zero,
        ],
        axis=0,
    )


def solution(mesh):
    in_specs = (P(("parts", "blk", "sub"), None), P(("parts", "blk", "sub")))
    out_specs = (P(("parts", "blk", "sub")), P("parts"))
    return jax.shard_map(per_device, mesh=mesh, in_specs=in_specs, out_specs=out_specs, check_vma=False)
```

```python
import functools
import math

import jax
import jax.numpy as jnp
from jax import lax
from jax.experimental import pallas as pl
from jax.experimental.pallas import tpu as pltpu
from jax.sharding import PartitionSpec as P

CLUSTERS = 128
TAU = 25.0
LOG2E = math.log2(math.e)
AXES = ("blk", "sub")
LANES = 128
VMEM = pl.BlockSpec(memory_space=pltpu.VMEM)
SMEM = pl.BlockSpec(memory_space=pltpu.SMEM)
PARAMS = pltpu.CompilerParams(vmem_limit_bytes=16 << 20)


def exchange(value, xor):
    count = lax.axis_size("blk") * lax.axis_size("sub")
    return lax.ppermute(value, AXES, [(i, i ^ xor) for i in range(count)])


def exchange_mixed(value):
    count = lax.axis_size("blk") * lax.axis_size("sub")
    return lax.ppermute(value, AXES, [(i, i ^ 3 if i & 1 else i ^ 5) for i in range(count)])


def down_rows(lab, first, size):
    pieces = []
    for at in range(first, first + size, LANES):
        n = min(LANES, first + size - at)
        pieces.append(jnp.broadcast_to(lab[:, at : at + n], (LANES, n)).T)
    return pieces[0] if len(pieces) == 1 else jnp.concatenate(pieces, axis=0)


def tile(rows, down, cols_ref, lab_ref, sum_ref, line, start, size, width, fold=True):
    scale = TAU * LOG2E / width
    folded = jnp.zeros((rows.shape[0], LANES), jnp.float32)
    for at in range(0, size, 256):
        n = min(256, size - at)
        score = lax.dot_general(
            rows, cols_ref[at : at + n, :], (((1,), (1,)), ((), ())), preferred_element_type=jnp.float32
        )
        power = jnp.exp2(score * scale - TAU * LOG2E)
        for lane in range(0, n, LANES):
            there = slice(start + at + lane, start + at + lane + LANES)
            value = jnp.where(down == lab_ref[:, there], power[:, lane : lane + LANES], 0.0)
            sum_ref[line : line + 1, there] = sum_ref[line : line + 1, there] + jnp.sum(value, axis=0, keepdims=True)
            if fold:
                folded = folded + value
    return folded


def to_lanes(folded):
    return jnp.sum(folded.T, axis=0, keepdims=True)


def split_kernel(source, *rest, spans):
    outs, sem = rest[:-1], rest[-1]
    copies = [
        pltpu.make_async_copy(source.at[pl.ds(at, n)], out, sem.at[i]) for i, ((at, n), out) in enumerate(zip(spans, outs))
    ]
    for copy in copies:
        copy.start()
    for copy in copies:
        copy.wait()


def split(source, spans):
    width = source.shape[1]
    return pl.pallas_call(
        functools.partial(split_kernel, spans=tuple(spans)),
        out_shape=[jax.ShapeDtypeStruct((n, width), source.dtype) for _, n in spans],
        in_specs=[pl.BlockSpec(memory_space=pltpu.HBM)],
        out_specs=[VMEM] * len(spans),
        scratch_shapes=[pltpu.SemaphoreType.DMA((len(spans),))],
        compiler_params=PARAMS,
        cost_estimate=pl.CostEstimate(flops=0, bytes_accessed=4 * width * sum(n for _, n in spans), transcendentals=0),
    )(source)


def near_kernel(*refs, width, chunks):
    parts = len(chunks)
    own, other = refs[:parts], refs[parts : 2 * parts]
    own_row, other_row, out_ref = refs[2 * parts :]
    out_ref[...] = jnp.zeros_like(out_ref)
    for pieces, lab in ((own, own_row), (other, other_row)):
        for rows, first, m in zip(pieces, starts(chunks), chunks):
            down = down_rows(lab, first, m)
            for piece, at, n in zip(own, starts(chunks), chunks):
                tile(rows[...], down, piece, own_row, out_ref, 0, at, n, width, False)


def starts(chunks):
    return [sum(chunks[:k]) for k in range(len(chunks))]


def near(own, other, own_row, other_row, chunks):
    width, count = own[0].shape[1], sum(chunks)
    return pl.pallas_call(
        functools.partial(near_kernel, width=width, chunks=tuple(chunks)),
        out_shape=jax.ShapeDtypeStruct((6, count), jnp.float32),
        in_specs=[VMEM] * (2 * len(own) + 2),
        out_specs=VMEM,
        compiler_params=PARAMS,
        cost_estimate=pl.CostEstimate(
            flops=4 * count * count * width, bytes_accessed=4 * count * width, transcendentals=2 * count * count
        ),
    )(*own, *other, own_row, other_row)


_, MET_FIRST, MET_SECOND, FIRST, SECOND, CROSS = range(6)


def far_kernel(*refs, width, chunks, news, ks, groups, line):
    parts = len(chunks)
    new, refs = refs[:news], refs[news:]
    cols = [refs[parts * g : parts * (g + 1)] for g in range(len(groups))]
    refs = refs[parts * len(groups) :]
    new_row, col_rows, (before, sums) = refs[0], refs[1 : 1 + len(groups)], refs[1 + len(groups) :]
    sums[...] = before[...]
    for piece, k in zip(new, ks):
        first, n = starts(chunks)[k], chunks[k]
        rows, down = piece[...], down_rows(new_row, first, n)
        fold = jnp.zeros((n, LANES), jnp.float32)
        for pieces, lab, met in zip(cols, col_rows, groups):
            for part, at, size in zip(pieces, starts(chunks), chunks):
                fold = fold + tile(rows, down, part, lab, sums, met, at, size, width)
        sums[line : line + 1, first : first + n] = sums[line : line + 1, first : first + n] + to_lanes(fold)


def far(new, ks, new_row, groups, sums, chunks, line):
    width, count = new[0].shape[1], sum(chunks)
    pairs = sum(chunks[k] for k in ks) * count * len(groups)
    cols = [piece for pieces, _, _ in groups for piece in pieces]
    return pl.pallas_call(
        functools.partial(
            far_kernel, width=width, chunks=tuple(chunks), news=len(new), ks=tuple(ks), groups=tuple(g[2] for g in groups), line=line
        ),
        out_shape=jax.ShapeDtypeStruct(sums.shape, jnp.float32),
        in_specs=[VMEM] * (len(new) + len(cols) + len(groups) + 2),
        out_specs=VMEM,
        compiler_params=PARAMS,
        cost_estimate=pl.CostEstimate(
            flops=2 * pairs * width, bytes_accessed=2 * width * count * (1 + len(groups)), transcendentals=pairs
        ),
    )(*new, *cols, new_row, *(g[1] for g in groups), sums)


CHUNKS = 3


def cut(count):
    base, more = divmod(count // LANES, CHUNKS)
    return [(base + (k < more)) * LANES for k in range(CHUNKS)]


def per_device(embeddings, labels):
    count, _ = embeddings.shape
    blk, sub = lax.axis_index("blk"), lax.axis_index("sub")
    chunks = cut(count)
    one = sub == 1
    low, high = blk & 1, (blk >> 1) & 1
    swapped, late = jnp.where(one, high, low) == 0, sub == high
    embeddings, labels, swapped, late, one, nil = lax.optimization_barrier((embeddings, labels, swapped, late, one, sub == 0))
    spans = list(zip(starts(chunks), chunks))
    first, second, cross = [], [], []
    own = [lax.slice_in_dim(embeddings, 0, chunks[0], axis=0)]
    first.append(exchange_mixed(own[0]))
    lab = labels[None, :]
    lab_other = exchange(lab, 1)
    lab_s = jnp.concatenate([lab, lab_other], axis=0)
    lab_x = exchange(lab_s, 2)
    lab_z = exchange(lab_s, 4)
    lab_d = exchange(lab_x, 4)
    source, _ = lax.optimization_barrier((embeddings, own[0]))
    own = own + list(split(source, spans[1:]))
    for k in range(1, len(chunks)):
        first.append(exchange_mixed(own[k]))
    partner = exchange(source, 1)
    other = split(partner, spans)
    for k in range(len(chunks)):
        second.append(exchange_mixed(other[k]))
    for k in range(len(chunks)):
        cross.append(exchange(first[k], 1))
    lab_all = jnp.concatenate([lab_s, lab_x, lab_z, lab_d], axis=0)
    first_lab, second_lab = jnp.where(one, lab_z[1:2], lab_x[1:2]), jnp.where(one, lab_z[0:1], lab_x[0:1])
    cross_lab = jnp.where(one, lab_x[0:1], lab_z[0:1])
    nobody = jnp.full_like(lab, -1)
    met_first = [jnp.where(swapped, b, a) for a, b in zip(own, other)]
    met_second = [jnp.where(swapped, a, b) for a, b in zip(own, other)]
    met_first_lab, met_second_lab = jnp.where(swapped, lab_other, lab), jnp.where(swapped, lab, lab_other)
    sums = near(own, other, lab, lab_other, chunks)
    for k in range(len(chunks)):
        sums = far(first[k : k + 1], [k], first_lab, [(met_first, met_first_lab, MET_FIRST)], sums, chunks, FIRST)
    early = [(cross, jnp.where(late, nobody, cross_lab), CROSS)]
    sums = far(first, range(len(chunks)), first_lab, early, sums, chunks, FIRST)
    meets = [(met_second, met_second_lab, MET_SECOND), (cross, jnp.where(late, cross_lab, nobody), CROSS)]
    for k in range(len(chunks)):
        sums = far(second[k : k + 1], [k], second_lab, meets, sums, chunks, SECOND)
    own_sum, met_a, met_b = sums[0:1], sums[1:2], sums[2:3]
    sums = jnp.concatenate(
        [own_sum + jnp.where(swapped, met_b, met_a), jnp.where(swapped, met_a, met_b), sums[3:6]], axis=0
    )
    part = spread(sums, one) + turned(spread(exchange(sums, 5), nil), 5)
    part = part + turned(exchange(part, 3), 3)
    part = part + turned(exchange(part, 1), 1)
    weight = 1.0 / part
    ident = jnp.arange(CLUSTERS, dtype=jnp.int32)
    mass = jnp.sum(jnp.where(lab_all[:, None, :] == ident[None, :, None], weight[:, None, :], 0.0), axis=(0, 2))
    bit = 8
    while bit < lax.axis_size("blk") * 2:
        mass = mass + exchange(mass, bit + 1)
        bit *= 2
    return weight[0], mass


def turned(rows, xor):
    return jnp.concatenate([rows[r ^ xor : (r ^ xor) + 1] for r in range(8)], axis=0)


def spread(sums, one):
    own, other, first, second, cross = (sums[r : r + 1] for r in range(5))
    zero = jnp.zeros_like(own)
    return jnp.concatenate(
        [
            own,
            other,
            jnp.where(one, cross, second),
            jnp.where(one, zero, first),
            jnp.where(one, second, cross),
            jnp.where(one, first, zero),
            zero,
            zero,
        ],
        axis=0,
    )


def solution(mesh):
    in_specs = (P(("parts", "blk", "sub"), None), P(("parts", "blk", "sub")))
    out_specs = (P(("parts", "blk", "sub")), P("parts"))
    return jax.shard_map(per_device, mesh=mesh, in_specs=in_specs, out_specs=out_specs, check_vma=False)
```
